512 devices in a mesh: seq: 32 (over z, core), mp: 16 (over y, x).
Axes of the slice: x: 4, y: 4, z: 16, core: 2. Of those that a mesh axis runs over, the one named last changes fastest.
Arguments:
- continued_prompt_entries: bfloat16 [4096, 4096], P('seq', 'mp'), may hold values from -6 to 6
- padded_prompt_entries: bfloat16 [4096, 4096], P('seq', 'mp'), may hold values from -6 to 6
- prompt_live_extents: int32 [64], P('seq'), may hold values from 8 to 64, as said below
- preceding_entry_line: bfloat16 [4096], P('mp'), may hold values from -6 to 6
- carried_memory: float32 [64, 64, 64], P('mp'), may hold values from -24 to 24
- token_mixing_ratios: float32 [5, 4096], replicated, may hold values from 0.05 to 0.95
- acceptance_transform: bfloat16 [4096, 4096], P('seq', 'mp'), may hold values from -0.09375 to 0.09375
- lookup_transform: bfloat16 [4096, 4096], P('seq', 'mp'), may hold values from -0.09375 to 0.09375
- payload_transform: bfloat16 [4096, 4096], P('seq', 'mp'), may hold values from -0.09375 to 0.09375
- gating_transform: bfloat16 [4096, 4096], P('seq', 'mp'), may hold values from -0.09375 to 0.09375
- fading_baseline: float32 [4096], P('mp'), may hold values from -10 to -3.5
- fading_left_factor: bfloat16 [4096, 128], replicated, may hold values from -0.09375 to 0.09375
- fading_right_factor: bfloat16 [128, 4096], P(None, 'mp'), may hold values from -0.5 to 0.5
- present_reward: float32 [64, 64], P('mp'), may hold values from -3 to 3
- group_layer_scaling: float32 [4096], P('mp'), may hold values from 0.5 to 1.5
- group_layer_shift_term: float32 [4096], P('mp'), may hold values from -1.8 to 1.8
- final_transform: bfloat16 [4096, 4096], P('mp', 'seq'), may hold values from -0.09375 to 0.09375
Outputs:
- mixed: bfloat16 [32, 256, 4096], P('seq', 'mp')
- span_states: float32 [32, 64, 64, 64], P('seq', 'mp')
- request_states: float32 [64, 64, 64, 64], P('seq', 'mp')
The draws below stay inside these ranges and needn't reach their ends.
Inputs may be any that keep to these rules, and one draw needn't show every extreme that they name: `prompt_live_extents`: some request has all 64 rows live.
All inputs are finite; a program needn't handle non-finite values.
Results may differ from the reference program's by a relative error of at most 0.0076.
Values may be sent and summed in bfloat16 or wider, within the bound.
A program may use at most 64 MiB of HBM per device.

```python
import jax
import jax.numpy as jnp
from jax import lax

D = 4096
ATTENTION_GROUPS = 64
CHANNEL_SPAN = 64
RANK = 128
L_DEV = 128
REQ_DEV = 2
SLOT = 64
GROUPS = 32
LONG = 4096
REQS = 64
SHORT = 4096


def draw_prompt_live_extents(key, part):
    lowest = max(1, SLOT // 8)
    drawn = jax.random.randint(key, (REQS,), lowest, SLOT + 1)
    drawn = drawn.at[0].set(SLOT)
    drawn = drawn.at[REQS - 1].set(lowest)
    return drawn.astype(jnp.int32)


def steps_of(rng, extent, shards, smallest, high):
    factor_of, own = 1.0, jax.random.fold_in(rng, 6)
    for axis_at, parts in shards:
        steps = jnp.exp(jax.random.uniform(jax.random.fold_in(own, axis_at), (parts,), jnp.float32, smallest / len(shards), high / len(shards)))
        factor_of = factor_of * jnp.repeat(steps, extent[axis_at] // parts).reshape([-1 if axis == axis_at else 1 for axis in range(len(extent))])
    return factor_of


def noise(stream_key, shape, deviation, most, split=(), kind=jnp.bfloat16):
    values = deviation * jax.random.normal(stream_key, shape, jnp.float32)
    if split:
        values = values * steps_of(stream_key, shape, split, -0.22, 0.18)
    return jnp.clip(values, -most, most).astype(kind)


def setup_inputs(seed: int = 0) -> dict:
    keys = jax.random.split(jax.random.key(seed), 18)
    return {
        "continued_prompt_entries": noise(keys[0], (LONG, D), 1.0, 6.0, ((0, 32), (1, 16))),
        "padded_prompt_entries": noise(keys[1], (SHORT, D), 1.0, 6.0, ((0, 32), (1, 16))),
        "prompt_live_extents": draw_prompt_live_extents(jax.random.fold_in(keys[17], 71), 0),
        "preceding_entry_line": noise(keys[3], (D,), 1.0, 6.0, ((0, 16),)),
        "carried_memory": noise(keys[4], (ATTENTION_GROUPS, CHANNEL_SPAN, CHANNEL_SPAN), 4.0, 24.0, ((0, 16),), jnp.float32),
        "token_mixing_ratios": jnp.clip(jax.random.uniform(keys[5], (5, D), jnp.float32, 0.05, 0.95), 0.05, 0.95),
        "acceptance_transform": noise(keys[6], (D, D), D ** -0.5, 0.09375, ((0, 32), (1, 16))),
        "lookup_transform": noise(keys[7], (D, D), D ** -0.5, 0.09375, ((0, 32), (1, 16))),
        "payload_transform": noise(keys[8], (D, D), D ** -0.5, 0.09375, ((0, 32), (1, 16))),
        "gating_transform": noise(keys[9], (D, D), D ** -0.5, 0.09375, ((0, 32), (1, 16))),
        "fading_baseline": jnp.clip(-10.0 + 6.5 * jax.random.uniform(keys[10], (D,), jnp.float32) ** steps_of(keys[10], (D,), ((0, 16),), -0.2, 0.2), -10.0, -3.5),
        "fading_left_factor": noise(keys[11], (D, RANK), D ** -0.5, 0.09375),
        "fading_right_factor": noise(keys[12], (RANK, D), RANK ** -0.5, 0.5, ((1, 16),)),
        "present_reward": noise(keys[13], (ATTENTION_GROUPS, CHANNEL_SPAN), 0.5, 3.0, ((0, 16),), jnp.float32),
        "group_layer_scaling": jnp.clip(1.0 + 0.1 * jax.random.normal(keys[14], (D,), jnp.float32), 0.5, 1.5),
        "group_layer_shift_term": noise(keys[15], (D,), 0.3, 1.8, ((0, 16),), jnp.float32),
        "final_transform": noise(keys[16], (D, D), D ** -0.5, 0.09375, ((0, 16), (1, 32))),
    }


def mix_rows(current, previous, weight):
    here = current.astype(jnp.float32)
    return (here + weight[None, :] * (previous.astype(jnp.float32) - here)).astype(jnp.bfloat16)

def reference(continued_prompt_entries, padded_prompt_entries, prompt_live_extents, preceding_entry_line, carried_memory, token_mixing_ratios, acceptance_transform, lookup_transform, payload_transform, gating_transform, fading_baseline, fading_left_factor, fading_right_factor, present_reward, group_layer_scaling, group_layer_shift_term, final_transform):
    long_prev = jnp.concatenate([preceding_entry_line[None, :], continued_prompt_entries[:-1]], axis=0)
    short_view = padded_prompt_entries.reshape(REQS, SLOT, D)
    short_prev = jnp.concatenate([jnp.zeros((REQS, 1, D), padded_prompt_entries.dtype), short_view[:, :-1]], axis=1).reshape(REQS * SLOT, D)
    current = jnp.concatenate([continued_prompt_entries, padded_prompt_entries], axis=0)
    previous = jnp.concatenate([long_prev, short_prev], axis=0)
    mixes = [mix_rows(current, previous, token_mixing_ratios[index]) for index in range(5)]
    acceptance_entries = jnp.dot(mixes[0], acceptance_transform, preferred_element_type=jnp.float32)
    lookup_entries = jnp.dot(mixes[1], lookup_transform, preferred_element_type=jnp.float32)
    payload_entries = jnp.dot(mixes[2], payload_transform, preferred_element_type=jnp.float32)
    gate = jnp.dot(mixes[3], gating_transform, preferred_element_type=jnp.float32)
    squeezed = jnp.tanh(jnp.dot(mixes[4], fading_left_factor, preferred_element_type=jnp.float32)).astype(jnp.bfloat16)
    log_fading_amount = -jnp.exp(fading_baseline[None, :] + jnp.dot(squeezed, fading_right_factor, preferred_element_type=jnp.float32))
    total_rows = LONG + SHORT
    heads_view = [a.reshape(total_rows, ATTENTION_GROUPS, CHANNEL_SPAN) for a in (acceptance_entries, lookup_entries, payload_entries, log_fading_amount)]

    def token_step(evolving_memory, entry_lines):
        acceptance_line, key_row, value_row, decay_row = entry_lines
        rank_one_update = key_row[:, :, None] * value_row[:, None, :]
        answer_lines = jnp.einsum('lr,lry->ly', acceptance_line, evolving_memory + present_reward[:, :, None] * rank_one_update, precision=lax.Precision.HIGHEST)
        return (jnp.exp(decay_row)[:, :, None] * evolving_memory + rank_one_update, answer_lines)

    def group_step(evolving_memory, entry_lines):
        evolving_memory, results = lax.scan(token_step, evolving_memory, entry_lines)
        return (evolving_memory, (results, evolving_memory))
    long_parts = tuple((a[:LONG].reshape(GROUPS, L_DEV, ATTENTION_GROUPS, CHANNEL_SPAN) for a in heads_view))
    final_state, (long_out, span_states) = lax.scan(group_step, carried_memory, long_parts)
    short_parts = tuple((a[LONG:].reshape(REQS, SLOT, ATTENTION_GROUPS, CHANNEL_SPAN) for a in heads_view))
    live_rows = lax.broadcasted_iota(jnp.int32, (REQS, SLOT), 1) < prompt_live_extents[:, None]

    def request_pass(acceptance_lines, lookup_table, payload_table, fading_table, live):

        def masked_step(evolving_memory, entry_lines):
            new_state, answer_lines = token_step(evolving_memory, entry_lines[:4])
            return (jnp.where(entry_lines[4], new_state, evolving_memory), answer_lines)
        return lax.scan(masked_step, jnp.zeros((ATTENTION_GROUPS, CHANNEL_SPAN, CHANNEL_SPAN), jnp.float32), (acceptance_lines, lookup_table, payload_table, fading_table, live))
    request_states, short_out = jax.vmap(request_pass)(*short_parts, live_rows)
    wkv = jnp.concatenate([long_out.reshape(LONG, ATTENTION_GROUPS, CHANNEL_SPAN), short_out.reshape(SHORT, ATTENTION_GROUPS, CHANNEL_SPAN)], axis=0)
    mean = lax.optimization_barrier(jnp.mean(wkv, axis=-1, keepdims=True))
    centred = wkv - mean
    variance = lax.optimization_barrier(jnp.mean(centred * centred, axis=-1, keepdims=True))
    normed = (centred * lax.rsqrt(variance + 0.00064)).reshape(total_rows, D) * group_layer_scaling[None, :] + group_layer_shift_term[None, :]
    row_live = jnp.concatenate([jnp.ones((LONG,), dtype=bool), live_rows.reshape(SHORT)], axis=0)
    hidden = jnp.where(row_live[:, None], normed * jax.nn.silu(gate), 0.0).astype(jnp.bfloat16)
    answer_lines = jnp.dot(hidden, final_transform, preferred_element_type=jnp.float32).astype(jnp.bfloat16)
    mixed = jnp.concatenate([answer_lines[:LONG].reshape(GROUPS, L_DEV, D), answer_lines[LONG:].reshape(GROUPS, REQ_DEV * SLOT, D)], axis=1)
    return (mixed, span_states, request_states)
```

```python
import jax
import jax.numpy as jnp
from jax import lax
from jax.sharding import PartitionSpec as P

BLK = 64
SEQ = ("z", "core")


norm_eps = 0.00064
highest = lax.Precision.HIGHEST


def seq_index():
    return lax.axis_index("z") * lax.axis_size("core") + lax.axis_index("core")


def seq_shift(x, by, length):
    pairs = [(i, i + by) for i in range(length) if i + by < length]
    return lax.ppermute(x, SEQ, pairs)


def exclusive_prefix(value, start, length):
    mine = seq_index()
    arrived = seq_shift(value, 1, length)
    total = jax.tree.map(lambda got, first: jnp.where(mine == 0, first, got), arrived, start)
    step = 1
    while step < length:
        got = seq_shift(total, step, length)
        joined = combine(got, total)
        total = jax.tree.map(lambda new, old: jnp.where(mine >= step, new, old), joined, total)
        step *= 2
    return total


def mix_rows(current, previous, weight):
    here = current.astype(jnp.float32)
    return (here + weight[None, :] * (previous.astype(jnp.float32) - here)).astype(jnp.bfloat16)


def block_sweep(
    evolving_memory,
    acceptance_entries,
    lookup_entries,
    payload_entries,
    log_fading_amount,
    diagonal_reward,
):
    inclusive = jnp.cumsum(log_fading_amount, axis=0)
    exclusive = inclusive - log_fading_amount
    recept_scaled = acceptance_entries * jnp.exp(exclusive)
    keys_scaled = lookup_entries * jnp.exp(-inclusive)
    scores = jnp.einsum("ihc,jhc->hij", recept_scaled, keys_scaled, precision=highest)
    count = acceptance_entries.shape[0]
    row_index = lax.broadcasted_iota(jnp.int32, (count, count), 0)
    col_index = lax.broadcasted_iota(jnp.int32, (count, count), 1)
    scores = jnp.where((row_index > col_index)[None], scores, 0.0)
    diagonal_contribution = jnp.sum(
        acceptance_entries * diagonal_reward[None] * lookup_entries, axis=-1, keepdims=True
    )
    answer_lines = (
        jnp.einsum("hij,jhd->ihd", scores, payload_entries, precision=highest)
        + diagonal_contribution * payload_entries
    )
    answer_lines = answer_lines + jnp.einsum(
        "ihc,hcd->ihd", recept_scaled, evolving_memory, precision=highest
    )
    total = inclusive[-1]
    carried = lookup_entries * jnp.exp(total[None] - inclusive)
    new_state = jnp.exp(total)[:, :, None] * evolving_memory + jnp.einsum(
        "jhc,jhd->hcd", carried, payload_entries, precision=highest
    )
    return (new_state, answer_lines)


def continued_recurrence(
    acceptance_entries, lookup_entries, payload_entries, log_fading_amount, diagonal_reward
):
    length, per_group_view, embedding_dimension = acceptance_entries.shape
    blocks = length // BLK

    def step(evolving_memory, entry_lines):
        return block_sweep(
            evolving_memory,
            entry_lines[0],
            entry_lines[1],
            entry_lines[2],
            entry_lines[3],
            diagonal_reward,
        )

    shaped = tuple(
        (
            a.reshape(blocks, BLK, per_group_view, embedding_dimension)
            for a in (acceptance_entries, lookup_entries, payload_entries, log_fading_amount)
        )
    )
    evolving_memory, results = lax.scan(
        step,
        jnp.zeros((per_group_view, embedding_dimension, embedding_dimension), jnp.float32),
        shaped,
    )
    return (evolving_memory, results.reshape(length, per_group_view, embedding_dimension))


def combine(earlier, later):
    return (earlier[0] + later[0], jnp.exp(later[0])[:, :, None] * earlier[1] + later[1])


def shifted_rows(current, edge_row, long_rows, requests, slot_rows):
    feature_part = current.shape[1]
    long_prev = jnp.concatenate([edge_row, current[: long_rows - 1]], axis=0)
    short_view = current[long_rows:].reshape(requests, slot_rows, feature_part)
    short_prev = jnp.concatenate(
        [jnp.zeros((requests, 1, feature_part), current.dtype), short_view[:, :-1]], axis=1
    )
    short_prev = short_prev.reshape(requests * slot_rows, feature_part)
    return jnp.concatenate([long_prev, short_prev], axis=0)


def on_device(
    continued_prompt_entries,
    padded_prompt_entries,
    prompt_live_extents,
    preceding_entry_line,
    carried_memory,
    token_mixing_ratios,
    acceptance_transform,
    lookup_transform,
    payload_transform,
    gating_transform,
    fading_baseline,
    fading_left_factor,
    fading_right_factor,
    present_reward,
    group_layer_scaling,
    group_layer_shift_term,
    final_transform,
):
    long_rows = continued_prompt_entries.shape[0]
    requests = prompt_live_extents.shape[0]
    slot_rows = padded_prompt_entries.shape[0] // requests
    per_group_view, embedding_dimension = present_reward.shape
    seq_count = lax.axis_size("z") * lax.axis_size("core")
    arrived = seq_shift(continued_prompt_entries[-1:], 1, seq_count)
    first = seq_index() == 0
    edge_row = jnp.where(first, preceding_entry_line[None, :], arrived)
    stacked = jnp.concatenate([continued_prompt_entries, padded_prompt_entries, edge_row], axis=0)
    stacked = lax.all_gather(stacked, "mp", axis=1, tiled=True)
    current = stacked[: long_rows + padded_prompt_entries.shape[0]]
    edge_full = stacked[-1:]
    previous = shifted_rows(current, edge_full, long_rows, requests, slot_rows)
    mixes = [mix_rows(current, previous, token_mixing_ratios[index]) for index in range(5)]
    total_rows = current.shape[0]
    columns = acceptance_transform.shape[1]
    blocks = jnp.stack(
        [acceptance_transform, lookup_transform, payload_transform, gating_transform, final_transform.T],
        axis=0,
    )
    blocks = lax.all_gather(lax.all_gather(blocks, "z"), "core")
    cores, chips, kinds, depth, width = blocks.shape
    blocks = jnp.transpose(blocks, (2, 1, 0, 3, 4)).reshape(kinds, chips * cores * depth, width)
    pieces = tuple(blocks[index] for index in range(4))
    acceptance_entries, lookup_entries, payload_entries, gate = tuple(
        (
            jnp.dot(source, piece, preferred_element_type=jnp.float32)
            for source, piece in zip(mixes[:4], pieces)
        )
    )
    squeezed = jnp.tanh(
        jnp.dot(mixes[4], fading_left_factor, preferred_element_type=jnp.float32)
    ).astype(jnp.bfloat16)
    log_fading_amount = -jnp.exp(
        fading_baseline[None, :]
        + jnp.dot(squeezed, fading_right_factor, preferred_element_type=jnp.float32)
    )
    recept3, keys3, values3, decay3 = [
        a.reshape(total_rows, per_group_view, embedding_dimension)
        for a in (acceptance_entries, lookup_entries, payload_entries, log_fading_amount)
    ]
    local_state, long_out = continued_recurrence(
        recept3[:long_rows],
        keys3[:long_rows],
        values3[:long_rows],
        decay3[:long_rows],
        present_reward,
    )
    long_decay = decay3[:long_rows]
    group_total = jnp.sum(long_decay, axis=0)
    start = (jnp.zeros((per_group_view, embedding_dimension), jnp.float32), carried_memory)
    _, incoming = exclusive_prefix((group_total, local_state), start, seq_count)
    before_row = jnp.cumsum(long_decay, axis=0) - long_decay
    long_out = long_out + jnp.einsum(
        "ihc,hcd->ihd", recept3[:long_rows] * jnp.exp(before_row), incoming, precision=highest
    )
    span_end = jnp.exp(group_total)[:, :, None] * incoming + local_state
    live_rows = (
        lax.broadcasted_iota(jnp.int32, (requests, slot_rows), 1) < prompt_live_extents[:, None]
    )
    live_flat = live_rows.reshape(requests * slot_rows).astype(jnp.float32)[:, None, None]
    short_shape = (requests, slot_rows, per_group_view, embedding_dimension)
    short_recept = recept3[long_rows:].reshape(short_shape)
    short_keys = (keys3[long_rows:] * live_flat).reshape(short_shape)
    short_values = values3[long_rows:].reshape(short_shape)
    short_decay = (decay3[long_rows:] * live_flat).reshape(short_shape)
    zeroed_memory = jnp.zeros(
        (per_group_view, embedding_dimension, embedding_dimension), jnp.float32
    )

    def request_pass(acceptance_lines, lookup_table, payload_table, fading_table):
        return block_sweep(
            zeroed_memory,
            acceptance_lines,
            lookup_table,
            payload_table,
            fading_table,
            present_reward,
        )

    request_states, short_out = jax.vmap(request_pass)(
        short_recept, short_keys, short_values, short_decay
    )
    wkv = jnp.concatenate(
        [long_out, short_out.reshape(requests * slot_rows, per_group_view, embedding_dimension)],
        axis=0,
    )
    mean = jnp.mean(wkv, axis=-1, keepdims=True)
    centred = wkv - mean
    variance = jnp.mean(centred * centred, axis=-1, keepdims=True)
    normed = (centred * lax.rsqrt(variance + norm_eps)).reshape(
        total_rows, columns
    ) * group_layer_scaling[None, :] + group_layer_shift_term[None, :]
    row_live = jnp.concatenate(
        [jnp.ones((long_rows,), dtype=bool), live_rows.reshape(requests * slot_rows)], axis=0
    )
    hidden = jnp.where(row_live[:, None], normed * jax.nn.silu(gate), 0.0).astype(jnp.bfloat16)
    full_out = blocks[4]
    mixed_rows = lax.psum_scatter(
        lax.dot_general(
            hidden, full_out, (((1,), (1,)), ((), ())), preferred_element_type=jnp.float32
        ),
        "mp",
        scatter_dimension=0,
        tiled=True,
    )
    return (mixed_rows.astype(jnp.bfloat16)[None], span_end[None], request_states)


def solution(mesh):
    placed = (
        P("seq", "mp"),
        P("seq", "mp"),
        P("seq"),
        P("mp"),
        P("mp", None, None),
        P(),
        P("seq", "mp"),
        P("seq", "mp"),
        P("seq", "mp"),
        P("seq", "mp"),
        P("mp"),
        P(),
        P(None, "mp"),
        P("mp", None),
        P("mp"),
        P("mp"),
        P("mp", "seq"),
    )
    devices = mesh.devices
    seq_devices, mp_devices = devices.shape
    mesh = jax.sharding.Mesh(devices.reshape(seq_devices // 2, 2, mp_devices), ("z", "core", "mp"))
    placed = tuple(
        P(*[SEQ if name == "seq" else name for name in spec]) for spec in placed
    )
    return jax.shard_map(
        on_device,
        mesh=mesh,
        in_specs=placed,
        out_specs=(P(SEQ, "mp", None), P(SEQ, "mp", None, None), P(SEQ, "mp", None, None)),
        check_vma=False,
    )
```
